32 devices in a mesh: cuts: 2 (over x), row: 16 (over z, y, core).
Axes of the slice: x: 2, y: 2, z: 4, core: 2. Of those that a mesh axis runs over, the one named last changes fastest.
Arguments:
- left_stem: bfloat16 [2, 8192, 4096], P(None, ('cuts', 'row')), parts along dimension 1, may hold values from -6 to 6
- right_stem: bfloat16 [2, 1024, 4096], P(None, ('cuts', 'row')), parts along dimension 1, may hold values from -6 to 6
- branches: bfloat16 [10, 2, 2, 512, 512], P(None, None, None, 'row'), may hold values from -0.1875 to 0.1875
- slice_bits: int32 [20], P('cuts'), parts along dimension 0, may hold values from 0 to 1
- perms: int32 [10, 8], P('cuts'), parts along dimension 0, may hold values from 0 to 7, each once within a row
Outputs:
- amplitude: float32 [2, 8192, 512], P(None, ('cuts', 'row')), parts along dimension 1
The draws below stay inside these ranges and needn't reach their ends.
There are 2 independent parts, one for each index of `cuts`. The reference program is written for one: setup_inputs(seed, part) draws one part's arguments, and reference() takes and returns one part's arrays. A program takes and returns all parts, laid end to end along the dimension named above; an argument that names none is the same for every part. Nothing has to cross between parts.
Inputs may be any that keep to these rules, and one draw needn't show every extreme that they name: `perms`: each row holds every group number once.
All inputs are finite; a program needn't handle non-finite values.
Results may differ from the reference program's by a relative error of at most 0.012.
Values may be sent and summed in bfloat16 or wider, within the bound.
No kernel may reach another device: no remote copies, remote signals or barrier semaphores. Data moves between devices by JAX's collectives and lax.ppermute only.
A program may use at most 64 MiB of HBM per device.

```python
import math
import jax
import jax.numpy as jnp

BR = 512
NBLK = 8
LROWS = 4096
RROWS = 512
LSWEEPS = 3
RSWEEPS = 2
COLS = 4096
NBR = 10


def place_ends(drawn, stream_key, least, top_value):
    shape = drawn.shape
    spot = [jax.random.randint(jax.random.fold_in(stream_key, axis), (), 0, shape[axis]) for axis in range(len(shape))]
    drawn = drawn.at[tuple(spot)].set(least)
    longest = shape.index(max(shape))
    spot[longest] = (spot[longest] + 1) % shape[longest]
    return drawn.at[tuple(spot)].set(top_value)


def block_scale(key, shape, split, low, high):
    loudness, own = 1.0, jax.random.fold_in(key, 6)
    for axis_at, parts in split:
        steps = jnp.exp(jax.random.uniform(jax.random.fold_in(own, axis_at), (parts,), jnp.float32, low / len(split), high / len(split)))
        loudness = loudness * jnp.repeat(steps, shape[axis_at] // parts).reshape([-1 if axis == axis_at else 1 for axis in range(len(shape))])
    return loudness


def scatter_about(key, shape, deviation, limit, cuts=(), kind=jnp.bfloat16):
    array = jax.random.normal(key, shape, jnp.float32) * deviation
    if len(cuts) > 0:
        array = block_scale(key, shape, cuts, -0.22, 0.18) * array
    return jnp.clip(array, min=-limit, max=limit).astype(kind)


def setup_inputs(seed: int = 0, part: int = 0) -> dict:
    streams_of = jax.random.split(jax.random.key(seed), 6)
    part_splits = jax.random.split(jax.random.fold_in(streams_of[5], part), 6)
    left_stem = scatter_about(part_splits[0], (2, LROWS, COLS), 1.0, 6.0, ((1, 16),))
    right_stem = scatter_about(part_splits[1], (2, RROWS, COLS), 1.0, 6.0, ((1, 16),))
    branches = scatter_about(streams_of[2], (NBR, 2, 2, BR, BR), (2 * BR) ** -0.5, 0.1875, ((3, 16),))
    slice_bits = place_ends(jax.random.randint(part_splits[3], (NBR,), 0, 2), jax.random.fold_in(part_splits[3], 1), 0, 1).astype(jnp.int32)
    perms = jax.vmap(lambda own: jax.random.permutation(own, NBLK))(jax.random.split(part_splits[4], (LSWEEPS + RSWEEPS))).reshape((LSWEEPS + RSWEEPS, NBLK)).astype(jnp.int32)
    return dict(left_stem=left_stem, right_stem=right_stem, branches=branches, slice_bits=slice_bits, perms=perms)


def column_mix(stem_in, matrix, strided):
    planes, rows, cols = stem_in.shape
    if strided:
        x_real = stem_in[0].astype(jnp.float32).reshape(rows, BR, cols // BR)
        x_imag = stem_in[1].astype(jnp.float32).reshape(rows, BR, cols // BR)
        p_real = matrix[0].astype(jnp.float32)
        p_imag = matrix[1].astype(jnp.float32)
        real_part = jnp.einsum('mcg,cd->mdg', x_real, p_real) - jnp.einsum('mcg,cd->mdg', x_imag, p_imag)
        imag_part = jnp.einsum('mcg,cd->mdg', x_real, p_imag) + jnp.einsum('mcg,cd->mdg', x_imag, p_real)
    else:
        x_real = stem_in[0].reshape(-1, BR)
        x_imag = stem_in[1].reshape(-1, BR)
        real_part = jnp.dot(x_real, matrix[0], preferred_element_type=jnp.float32) - jnp.dot(x_imag, matrix[1], preferred_element_type=jnp.float32)
        imag_part = jnp.dot(x_real, matrix[1], preferred_element_type=jnp.float32) + jnp.dot(x_imag, matrix[0], preferred_element_type=jnp.float32)
    return jnp.stack([real_part, imag_part]).reshape(planes, rows, cols).astype(jnp.bfloat16)

def row_mix(stem_in, matrix, strided):
    planes, rows, cols = stem_in.shape
    groups = rows // BR
    q_real = matrix[0].astype(jnp.float32)
    q_imag = matrix[1].astype(jnp.float32)
    if strided:
        y_real = stem_in[0].astype(jnp.float32).reshape(BR, groups, cols)
        y_imag = stem_in[1].astype(jnp.float32).reshape(BR, groups, cols)
        form = 'rs,sgn->rgn'
    else:
        y_real = stem_in[0].astype(jnp.float32).reshape(groups, BR, cols)
        y_imag = stem_in[1].astype(jnp.float32).reshape(groups, BR, cols)
        form = 'rs,hsn->hrn'
    real_part = jnp.einsum(form, q_real, y_real) - jnp.einsum(form, q_imag, y_imag)
    imag_part = jnp.einsum(form, q_real, y_imag) + jnp.einsum(form, q_imag, y_real)
    return jnp.stack([real_part, imag_part]).reshape(planes, rows, cols).astype(jnp.bfloat16)

def permute(stem_in, block_order):
    planes, rows, cols = stem_in.shape
    blocked = stem_in.reshape(planes, rows, NBLK, BR)
    return jnp.take(blocked, block_order, axis=2).reshape(planes, rows, cols)

def reference(left_stem, right_stem, branches, slice_bits, perms):
    chosen = branches[jnp.arange(NBR, dtype=jnp.int32), slice_bits]
    left = left_stem
    for sweep in range(LSWEEPS):
        strided = sweep % 2 == 1
        left = permute(row_mix(column_mix(left, chosen[2 * sweep], strided), chosen[2 * sweep + 1], strided), perms[sweep])
    right = right_stem
    for sweep in range(LSWEEPS, LSWEEPS + RSWEEPS):
        strided = sweep % 2 == 1
        right = permute(row_mix(column_mix(right, chosen[2 * sweep], strided), chosen[2 * sweep + 1], strided), perms[sweep])
    scale = 1.0 / math.sqrt(2.0 * COLS)
    real_part = jnp.dot(left[0], right[0].T, preferred_element_type=jnp.float32) - jnp.dot(left[1], right[1].T, preferred_element_type=jnp.float32)
    imag_part = jnp.dot(left[0], right[1].T, preferred_element_type=jnp.float32) + jnp.dot(left[1], right[0].T, preferred_element_type=jnp.float32)
    return jnp.stack([real_part, imag_part]) * scale
```

```python
import functools

import jax
import jax.numpy as jnp
import numpy as np
from jax import lax
from jax.experimental import pallas as pl
from jax.experimental.pallas import tpu as pltpu
from jax.sharding import PartitionSpec as P


LEFT_SWEEPS = 3
RIGHT_SWEEPS = 2
F32 = jnp.float32
BF16 = jnp.bfloat16
NN = (((1,), (0,)), ((), ()))
NT = (((1,), (1,)), ((), ()))


def ring_order(mesh):
    devices = list(mesh.devices.reshape(-1, mesh.shape["row"])[0])
    chips = len(devices) // 2
    natural = list(range(chips))
    try:
        coords = [tuple(d.coords) for d in devices]
    except AttributeError:
        return natural
    spots = coords[::2]
    axes = [a for a in range(len(spots[0])) if len({s[a] for s in spots}) > 1]
    if len(axes) != 2:
        return natural
    short, long = sorted(axes, key=lambda a: len({s[a] for s in spots}))
    values = sorted({s[short] for s in spots})
    if len(values) != 2:
        return natural
    up = sorted((c for c in natural if spots[c][short] == values[0]), key=lambda c: spots[c][long])
    down = sorted((c for c in natural if spots[c][short] == values[1]), key=lambda c: -spots[c][long])
    return up + down


class Ring:
    def __init__(self, mesh):
        order = ring_order(mesh)
        self.chips = len(order)
        n = self.chips
        self.hop = [(2 * order[i], 2 * order[(i + 1) % n]) for i in range(n)]
        self.hop += [(2 * order[i] + 1, 2 * order[(i - 1) % n] + 1) for i in range(n)]
        self.swap = [(i, i ^ 1) for i in range(2 * n)]
        place = {chip: i for i, chip in enumerate(order)}
        table = np.zeros((2 * n, 2 * n), np.int32)
        for device in range(2 * n):
            chip, core = divmod(device, 2)
            for other in range(2):
                source = core ^ other
                sign = -1 if source == 0 else 1
                for step in range(n):
                    table[device, other * n + step] = 2 * order[(place[chip] + sign * step) % n] + source
        self.table = table

    def owners(self):
        return jnp.asarray(self.table)[lax.axis_index("row")]

    def same_core(self, shard):
        pieces = [shard]
        for _ in range(self.chips - 1):
            pieces.append(lax.ppermute(pieces[-1], "row", self.hop))
        return pieces

    def gather(self, shard):
        pieces = self.same_core(shard)
        return pieces + [lax.ppermute(p, "row", self.swap) for p in pieces]


def mix(x, matrix, transposed, strided):
    planes, rows, cols = x.shape
    width = matrix.shape[-1]
    groups = cols // width
    second = "dc" if transposed else "cd"
    if strided:
        view, form = x.reshape(planes, rows, width, groups), f"mcg,{second}->mdg"
    else:
        view, form = x.reshape(planes, rows, groups, width), f"mgc,{second}->mgd"

    def product(a, b):
        return jnp.einsum(form, a, b, preferred_element_type=F32)

    real_part = product(view[0], matrix[0]) - product(view[1], matrix[1])
    imag_part = product(view[0], matrix[1]) + product(view[1], matrix[0])
    return jnp.stack([real_part, imag_part]).reshape(x.shape).astype(BF16)


def permute(x, block_order):
    planes, rows, cols = x.shape
    blocks = block_order.shape[0]
    return jnp.take(x.reshape(planes, rows, blocks, cols // blocks), block_order, axis=2).reshape(x.shape)


def assemble(pieces, owners):
    order = jnp.zeros_like(owners).at[owners].set(jnp.arange(owners.shape[0], dtype=owners.dtype))
    stacked = jnp.take(jnp.stack(pieces), order, axis=0)
    count, matrices, planes, rows, width = stacked.shape
    return stacked.transpose(1, 2, 0, 3, 4).reshape(matrices, planes, count * rows, width)


def shards(ring, left_stem, right_stem, branches, slice_bits, perms):
    cols = left_stem.shape[2]
    chips = ring.chips
    owners = ring.owners()
    pick = (slice_bits == 0)[:, None, None, None]
    chosen = jnp.where(pick, branches[:, 0], branches[:, 1])

    col_mats = jnp.stack([chosen[i] for i in (6, 8, 4, 2, 0)])
    row_mats = jnp.stack([chosen[i] for i in (1, 3, 5)])
    join_mats = jnp.stack([chosen[i] for i in (7, 9)])

    left_other = lax.ppermute(left_stem, "row", ring.swap)
    mats = assemble(ring.gather(col_mats), owners)
    inverse = jnp.argsort(perms, axis=1)
    v = mix(right_stem, mats[0], False, True)
    v = permute(v, perms[3])
    v = mix(v, mats[1], False, False)
    v = permute(v, perms[4])
    v = permute(v, inverse[2])
    v = mix(v, mats[2], True, False)
    v = permute(v, inverse[1])
    v = mix(v, mats[3], True, True)
    v = permute(v, inverse[0])
    v = mix(v, mats[4], True, False)

    pieces = ring.same_core(v)
    core = lax.axis_index("row") % 2
    first = jnp.where(core == 0, left_stem, left_other)
    second = jnp.where(core == 0, left_other, left_stem)
    left = jnp.concatenate([first, second], axis=1)
    order = jnp.zeros((chips,), jnp.int32).at[owners[:chips] // 2].set(jnp.arange(chips, dtype=jnp.int32))
    right = jnp.take(jnp.stack(pieces), order, axis=0)

    def product(a, b):
        return jnp.einsum("qjk,ik->qji", a, b, preferred_element_type=F32)

    real_part = product(right[:, 0], left[0]) - product(right[:, 1], left[1])
    imag_part = product(right[:, 0], left[1]) + product(right[:, 1], left[0])
    joined = jnp.stack([real_part, imag_part], axis=1).astype(BF16)
    groups = [list(range(c, 2 * chips, 2)) for c in range(2)]
    spread = lax.all_to_all(joined, "row", 0, 0, axis_index_groups=groups, tiled=True)
    t = spread.transpose(1, 2, 0, 3).reshape(2, spread.shape[2], -1)
    row_full = assemble(ring.gather(row_mats), owners)
    t = mix(t, row_full[0], True, False)
    t = mix(t, row_full[1], True, True)
    t = mix(t, row_full[2], True, False)
    back = t.reshape(2, t.shape[1], 2 * chips, -1).transpose(2, 0, 1, 3)
    back = lax.all_to_all(back, "row", 0, 0, tiled=True)
    t = back.transpose(1, 0, 2, 3).reshape(2, -1, back.shape[3])
    join_full = assemble(ring.gather(join_mats), owners)

    def apply(form, m, y):
        def p(a, b):
            return jnp.einsum(form, a, b, preferred_element_type=F32)

        return jnp.stack([p(m[0], y[0]) - p(m[1], y[1]), p(m[0], y[1]) + p(m[1], y[0])])

    t = apply("lj,ji->li", join_full[0], t).astype(BF16)
    out = apply("lj,ji->il", join_full[1], t)
    return out * (2.0 * cols) ** (-0.5)


def solution(mesh):
    in_specs = (
        P(None, ("cuts", "row"), None),
        P(None, ("cuts", "row"), None),
        P(None, None, None, "row", None),
        P("cuts"),
        P("cuts", None),
    )
    out_specs = P(None, ("cuts", "row"), None)
    body = functools.partial(shards, Ring(mesh))
    return jax.shard_map(body, mesh=mesh, in_specs=in_specs, out_specs=out_specs, check_vma=False)
```

```python
import functools

import jax
import jax.numpy as jnp
import numpy as np
from jax import lax
from jax.experimental import pallas as pl
from jax.experimental.pallas import tpu as pltpu
from jax.sharding import PartitionSpec as P


LEFT_SWEEPS = 3
RIGHT_SWEEPS = 2
F32 = jnp.float32
BF16 = jnp.bfloat16
NN = (((1,), (0,)), ((), ()))
NT = (((1,), (1,)), ((), ()))


def ring_order(mesh):
    devices = list(mesh.devices.reshape(-1, mesh.shape["row"])[0])
    chips = len(devices) // 2
    natural = list(range(chips))
    try:
        coords = [tuple(d.coords) for d in devices]
    except AttributeError:
        return natural
    spots = coords[::2]
    axes = [a for a in range(len(spots[0])) if len({s[a] for s in spots}) > 1]
    if len(axes) != 2:
        return natural
    short, long = sorted(axes, key=lambda a: len({s[a] for s in spots}))
    values = sorted({s[short] for s in spots})
    if len(values) != 2:
        return natural
    up = sorted((c for c in natural if spots[c][short] == values[0]), key=lambda c: spots[c][long])
    down = sorted((c for c in natural if spots[c][short] == values[1]), key=lambda c: -spots[c][long])
    return up + down


class Ring:
    def __init__(self, mesh):
        order = ring_order(mesh)
        self.chips = len(order)
        n = self.chips
        self.hop = [(2 * order[i], 2 * order[(i + 1) % n]) for i in range(n)]
        self.hop += [(2 * order[i] + 1, 2 * order[(i - 1) % n] + 1) for i in range(n)]
        self.swap = [(i, i ^ 1) for i in range(2 * n)]
        place = {chip: i for i, chip in enumerate(order)}
        table = np.zeros((2 * n, 2 * n), np.int32)
        for device in range(2 * n):
            chip, core = divmod(device, 2)
            for other in range(2):
                source = core ^ other
                sign = -1 if source == 0 else 1
                for step in range(n):
                    table[device, other * n + step] = 2 * order[(place[chip] + sign * step) % n] + source
        self.table = table

    def owners(self):
        return jnp.asarray(self.table)[lax.axis_index("row")]

    def same_core(self, shard):
        pieces = [shard]
        for _ in range(self.chips - 1):
            pieces.append(lax.ppermute(pieces[-1], "row", self.hop))
        return pieces

    def gather(self, shard):
        pieces = self.same_core(shard)
        return pieces + [lax.ppermute(p, "row", self.swap) for p in pieces]


def mix(x, matrix, transposed, strided):
    planes, rows, cols = x.shape
    width = matrix.shape[-1]
    groups = cols // width
    second = "dc" if transposed else "cd"
    if strided:
        view, form = x.reshape(planes, rows, width, groups), f"mcg,{second}->mdg"
    else:
        view, form = x.reshape(planes, rows, groups, width), f"mgc,{second}->mgd"

    def product(a, b):
        return jnp.einsum(form, a, b, preferred_element_type=F32)

    real_part = product(view[0], matrix[0]) - product(view[1], matrix[1])
    imag_part = product(view[0], matrix[1]) + product(view[1], matrix[0])
    return jnp.stack([real_part, imag_part]).reshape(x.shape).astype(BF16)


def permute(x, block_order):
    planes, rows, cols = x.shape
    blocks = block_order.shape[0]
    return jnp.take(x.reshape(planes, rows, blocks, cols // blocks), block_order, axis=2).reshape(x.shape)


def assemble(pieces, owners):
    order = jnp.zeros_like(owners).at[owners].set(jnp.arange(owners.shape[0], dtype=owners.dtype))
    stacked = jnp.take(jnp.stack(pieces), order, axis=0)
    count, matrices, planes, rows, width = stacked.shape
    return stacked.transpose(1, 2, 0, 3, 4).reshape(matrices, planes, count * rows, width)


def rows_of(plane, group, groups, rows):
    return (plane * groups + group) * rows


def lane_order(width, groups):
    source = lax.broadcasted_iota(jnp.int32, (width, width), 0)
    target = lax.broadcasted_iota(jnp.int32, (width, width), 1)
    sub = width // groups
    wanted = lax.rem(target, sub) * groups + lax.div(target, sub)
    return (source == wanted).astype(F32).astype(BF16)


def exchange_digits(src, dst, groups, rows, index=None):
    lane = lax.broadcasted_iota(jnp.int32, (rows, 128), 1)
    low = lane < 64

    def start(plane, group):
        if index is None:
            return rows_of(plane, group, groups, rows)
        return pl.multiple_of(plane * groups * rows + index(group) * rows, rows)

    for plane in range(2):
        for a in range(groups // 2):
            for b in range(groups // 2):
                even = src[pl.ds(start(plane, 2 * a), rows), b * 128 : (b + 1) * 128]
                odd = src[pl.ds(start(plane, 2 * a + 1), rows), b * 128 : (b + 1) * 128]
                lanes = slice(a * 128, (a + 1) * 128)
                first = rows_of(plane, 2 * b, groups, rows)
                dst[first : first + rows, lanes] = jnp.where(low, even, pltpu.roll(odd, 64, 1))
                second = rows_of(plane, 2 * b + 1, groups, rows)
                dst[second : second + rows, lanes] = jnp.where(low, pltpu.roll(even, 64, 1), odd)


def complex_mix(src, dst, mats, index, transposed):
    half = src.shape[0] // 2
    x = src[...].astype(BF16)
    turned = jnp.concatenate([-x[half:], x[:half]], axis=0)
    dims = NT if transposed else NN
    dst[...] = lax.dot_general(x, mats[index, 0], dims, preferred_element_type=F32) + lax.dot_general(
        turned, mats[index, 1], dims, preferred_element_type=F32
    )


def reorder(src, dst, order, transposed):
    dims = NT if transposed else NN
    dst[...] = lax.dot_general(src[...].astype(BF16), order[...], dims, preferred_element_type=F32)


def load_matrices(pieces, owners, mats, sems, rows):
    copies = []
    for plane, group in enumerate(pieces):
        for at, piece in enumerate(group):
            where = pl.ds(pl.multiple_of(owners[at] * rows, rows), rows)
            copy = pltpu.make_async_copy(piece, mats.at[:, plane, where, :], sems.at[plane, at])
            copy.start()
            copies.append(copy)
    return copies


def right_kernel(count, owners, perms, x, *refs):
    pieces = [refs[:count], refs[count : 2 * count]]
    out_real, out_imag, mats, a, b, order, inverse, sems = refs[2 * count :]
    planes, rows, cols = x.shape
    width = order.shape[0]
    groups = cols // width
    copies = load_matrices(pieces, owners, mats, sems, width // count)
    order[...] = lane_order(width, groups)
    for sweep in range(LEFT_SWEEPS):
        for g in range(groups):
            inverse[sweep, perms[sweep, g]] = g
    for plane in range(planes):
        for g in range(groups):
            at = rows_of(plane, g, groups, rows)
            a[at : at + rows, :] = x[plane, :, g * width : (g + 1) * width].astype(F32)
    reorder(a, b, order, False)
    exchange_digits(b, a, groups, rows)
    for copy in copies:
        copy.wait()
    complex_mix(a, b, mats, 0, False)
    exchange_digits(b, a, groups, rows)
    reorder(a, b, order, True)
    complex_mix(b, a, mats, 1, False)
    complex_mix(a, b, mats, 2, True)
    reorder(b, a, order, False)

    def block(group):
        return perms[LEFT_SWEEPS, perms[LEFT_SWEEPS + 1, inverse[2, inverse[1, group]]]]

    exchange_digits(a, b, groups, rows, block)
    complex_mix(b, a, mats, 3, True)
    exchange_digits(a, b, groups, rows)
    reorder(b, a, order, True)
    complex_mix(a, b, mats, 4, True)
    for plane, out in enumerate((out_real, out_imag)):
        for g in range(groups):
            at = pl.multiple_of(plane * groups * rows + inverse[0, g] * rows, rows)
            out[:, g * width : (g + 1) * width] = b[pl.ds(at, rows), :].astype(BF16)


def row_kernel(count, owners, x, *refs):
    pieces = [refs[:count], refs[count : 2 * count]]
    out, mats, a, b, order, sems = refs[2 * count :]
    groups, planes, rows, width = x.shape
    copies = load_matrices(pieces, owners, mats, sems, width // count)
    order[...] = lane_order(width, groups)
    for plane in range(planes):
        for g in range(groups):
            at = rows_of(plane, g, groups, rows)
            a[at : at + rows, :] = x[g, plane].astype(F32)
    for copy in copies:
        copy.wait()
    complex_mix(a, b, mats, 0, True)
    reorder(b, a, order, False)
    exchange_digits(a, b, groups, rows)
    complex_mix(b, a, mats, 1, True)
    exchange_digits(a, b, groups, rows)
    reorder(b, a, order, True)
    complex_mix(a, b, mats, 2, True)
    half = width // 2
    for plane in range(planes):
        for g in range(groups):
            at = rows_of(plane, g, groups, rows)
            for part in range(2):
                out[2 * g + part, plane] = b[at : at + rows, part * half : (part + 1) * half].astype(BF16)


def join_kernel(chips, owners, own, other, *refs):
    pieces = [refs[:chips], refs[chips : 2 * chips]]
    out, lhs, total = refs[2 * chips :]
    step = pl.program_id(0)
    rows = pieces[0][0].shape[0]
    height = chips * rows
    for at in range(chips):
        real, imag = pieces[0][at][...], pieces[1][at][...]
        lhs[0, at * rows : (at + 1) * rows, :] = real
        lhs[0, height + at * rows : height + (at + 1) * rows, :] = imag
        lhs[1, at * rows : (at + 1) * rows, :] = -imag
        lhs[1, height + at * rows : height + (at + 1) * rows, :] = real

    def product(stem):
        return lax.dot_general(lhs[0], stem[0], NT, preferred_element_type=F32) + lax.dot_general(
            lhs[1], stem[1], NT, preferred_element_type=F32
        )

    @pl.when(step == 0)
    def _():
        total[...] = jnp.zeros_like(total)

    total[0] += product(own)
    total[1] += product(other)

    @pl.when(step == pl.num_programs(0) - 1)
    def _():
        core = lax.rem(owners[0], 2)
        width = own.shape[1]
        for at in range(chips):
            owner = lax.div(owners[at], 2)
            for plane in range(2):
                first = plane * height + at * rows
                mine = total[0, first : first + rows, :].astype(BF16)
                theirs = total[1, first : first + rows, :].astype(BF16)
                out[owner, plane, :, :width] = jnp.where(core == 0, mine, theirs)
                out[owner, plane, :, width:] = jnp.where(core == 0, theirs, mine)


def last_kernel(count, scale, owners, x, *refs):
    pieces = [refs[:count], refs[count : 2 * count]]
    out, mats, a, b, sems = refs[2 * count :]
    _, planes, rows, width = x.shape
    copies = load_matrices(pieces, owners, mats, sems, mats.shape[2] // count)
    for plane in range(planes):
        for at in range(count):
            b[at * rows : (at + 1) * rows, plane * width : (plane + 1) * width] = x[at, plane].astype(F32)
    a[...] = b[...].T
    for copy in copies:
        copy.wait()
    complex_mix(a, b, mats, 0, True)
    complex_mix(b, a, mats, 1, True)
    for plane in range(planes):
        out[plane] = a[plane * width : (plane + 1) * width, :] * scale


SMEM = pl.BlockSpec(memory_space=pltpu.SMEM)
VMEM = pl.BlockSpec(memory_space=pltpu.VMEM)
ANY = pl.BlockSpec(memory_space=pl.ANY)


def kernel_params():
    return pltpu.CompilerParams(vmem_limit_bytes=48 * 1024 * 1024)


def estimate(flops, nbytes):
    return pl.CostEstimate(flops=int(flops), bytes_accessed=int(nbytes), transcendentals=0)


def mix_right(owners, perms, x, real, imag):
    count = len(real)
    matrices, rows, width = real[0].shape
    planes, height, cols = x.shape
    tall = planes * height * cols // width
    return pl.pallas_call(
        functools.partial(right_kernel, count),
        out_shape=[jax.ShapeDtypeStruct((height, cols), BF16)] * 2,
        in_specs=[SMEM, SMEM, VMEM] + [ANY] * (2 * count),
        out_specs=[VMEM, VMEM],
        scratch_shapes=[
            pltpu.VMEM((matrices, 2, width, width), BF16),
            pltpu.VMEM((tall, width), F32),
            pltpu.VMEM((tall, width), F32),
            pltpu.VMEM((width, width), BF16),
            pltpu.SMEM((LEFT_SWEEPS, cols // width), jnp.int32),
            pltpu.SemaphoreType.DMA((2, count)),
        ],
        cost_estimate=estimate(4 * tall * width * width * matrices * 2, 2 * matrices * 2 * width * width),
        compiler_params=kernel_params(),
        name="mix_right",
    )(owners, perms, x, *real, *imag)


def mix_rows(owners, x, real, imag):
    count = len(real)
    matrices, rows, width = real[0].shape
    groups, planes, height, _ = x.shape
    tall = planes * height * groups
    return pl.pallas_call(
        functools.partial(row_kernel, count),
        out_shape=jax.ShapeDtypeStruct((2 * groups, planes, height, width // 2), BF16),
        in_specs=[SMEM, VMEM] + [ANY] * (2 * count),
        out_specs=VMEM,
        scratch_shapes=[
            pltpu.VMEM((matrices, 2, width, width), BF16),
            pltpu.VMEM((tall, width), F32),
            pltpu.VMEM((tall, width), F32),
            pltpu.VMEM((width, width), BF16),
            pltpu.SemaphoreType.DMA((2, count)),
        ],
        cost_estimate=estimate(4 * tall * width * width * matrices * 2, 2 * matrices * 2 * width * width),
        compiler_params=kernel_params(),
        name="mix_rows",
    )(owners, x, *real, *imag)


def join(owners, own, other, real, imag):
    chips = len(real)
    rows, cols = real[0].shape
    height = own.shape[1]
    depth = 512
    piece = pl.BlockSpec((rows, depth), lambda k: (0, k))
    stem = pl.BlockSpec((2, height, depth), lambda k: (0, 0, k))
    return pl.pallas_call(
        functools.partial(join_kernel, chips),
        grid=(cols // depth,),
        out_shape=jax.ShapeDtypeStruct((chips, 2, rows, 2 * height), BF16),
        in_specs=[SMEM, stem, stem] + [piece] * (2 * chips),
        out_specs=pl.BlockSpec((chips, 2, rows, 2 * height), lambda k: (0, 0, 0, 0)),
        scratch_shapes=[
            pltpu.VMEM((2, 2 * chips * rows, depth), BF16),
            pltpu.VMEM((2, 2 * chips * rows, height), F32),
        ],
        cost_estimate=estimate(16 * chips * rows * cols * height, 2 * 2 * cols * (2 * height + chips * rows)),
        compiler_params=kernel_params(),
        name="join",
    )(owners, own, other, *real, *imag)


def mix_last(owners, scale, x, real, imag):
    count = len(real)
    matrices, rows, full = real[0].shape
    _, planes, _, width = x.shape
    return pl.pallas_call(
        functools.partial(last_kernel, count, scale),
        out_shape=jax.ShapeDtypeStruct((planes, width, full), F32),
        in_specs=[SMEM, VMEM] + [ANY] * (2 * count),
        out_specs=VMEM,
        scratch_shapes=[
            pltpu.VMEM((matrices, 2, full, full), BF16),
            pltpu.VMEM((planes * width, full), F32),
            pltpu.VMEM((full, planes * width), F32),
            pltpu.SemaphoreType.DMA((2, count)),
        ],
        cost_estimate=estimate(4 * planes * width * full * full * matrices, 2 * matrices * 2 * full * full),
        compiler_params=kernel_params(),
        name="mix_last",
    )(owners, x, *real, *imag)


def fits_kernels(ring, left_stem, right_stem, branches):
    rows, width = branches.shape[3:]
    groups = left_stem.shape[2] // width
    return (
        rows % 16 == 0
        and right_stem.shape[1] % 16 == 0
        and 2 * left_stem.shape[1] == width
        and ring.chips == groups
        and width // groups == 64
        and groups % 2 == 0
        and 2 * ring.chips * right_stem.shape[1] == width
    )


def shards(ring, left_stem, right_stem, branches, slice_bits, perms):
    if fits_kernels(ring, left_stem, right_stem, branches):
        return shards_kernels(ring, left_stem, right_stem, branches, slice_bits, perms)
    return shards_xla(ring, left_stem, right_stem, branches, slice_bits, perms)


def shards_kernels(ring, left_stem, right_stem, branches, slice_bits, perms):
    cols = left_stem.shape[2]
    chips = ring.chips
    owners = ring.owners()

    def chosen(plane, indices):
        return jnp.stack(
            [jnp.where(slice_bits[i] == 0, branches[i, 0, plane], branches[i, 1, plane]) for i in indices]
        )

    def gather(indices, after=None):
        shards = [chosen(plane, indices) for plane in range(2)]
        if after is not None:
            *shards, _ = lax.optimization_barrier((*shards, after))
        return [ring.gather(shard) for shard in shards]

    left_other = lax.ppermute(left_stem, "row", ring.swap)
    col_pieces = gather((6, 8, 4, 2, 0))
    late = col_pieces[1][chips - 1]
    row_pieces = gather((1, 3, 5), late)
    join_pieces = gather((7, 9), late)
    shard = mix_right(owners, perms, right_stem, *col_pieces)
    right = [ring.same_core(plane) for plane in shard]
    joined = join(owners[:chips], left_stem, left_other, *right)
    groups = [list(range(c, 2 * chips, 2)) for c in range(2)]
    spread = lax.all_to_all(joined, "row", 0, 0, axis_index_groups=groups, tiled=True)
    mixed = mix_rows(owners, spread, *row_pieces)
    back = lax.all_to_all(mixed, "row", 0, 0, tiled=True)
    return mix_last(owners, (2.0 * cols) ** (-0.5), back, *join_pieces)


def shards_xla(ring, left_stem, right_stem, branches, slice_bits, perms):
    cols = left_stem.shape[2]
    chips = ring.chips
    owners = ring.owners()
    pick = (slice_bits == 0)[:, None, None, None]
    chosen = jnp.where(pick, branches[:, 0], branches[:, 1])

    col_mats = jnp.stack([chosen[i] for i in (6, 8, 4, 2, 0)])
    row_mats = jnp.stack([chosen[i] for i in (1, 3, 5)])
    join_mats = jnp.stack([chosen[i] for i in (7, 9)])

    left_other = lax.ppermute(left_stem, "row", ring.swap)
    mats = assemble(ring.gather(col_mats), owners)
    inverse = jnp.argsort(perms, axis=1)
    v = mix(right_stem, mats[0], False, True)
    v = permute(v, perms[3])
    v = mix(v, mats[1], False, False)
    v = permute(v, perms[4])
    v = permute(v, inverse[2])
    v = mix(v, mats[2], True, False)
    v = permute(v, inverse[1])
    v = mix(v, mats[3], True, True)
    v = permute(v, inverse[0])
    v = mix(v, mats[4], True, False)

    pieces = ring.same_core(v)
    core = lax.axis_index("row") % 2
    first = jnp.where(core == 0, left_stem, left_other)
    second = jnp.where(core == 0, left_other, left_stem)
    left = jnp.concatenate([first, second], axis=1)
    order = jnp.zeros((chips,), jnp.int32).at[owners[:chips] // 2].set(jnp.arange(chips, dtype=jnp.int32))
    right = jnp.take(jnp.stack(pieces), order, axis=0)

    def product(a, b):
        return jnp.einsum("qjk,ik->qji", a, b, preferred_element_type=F32)

    real_part = product(right[:, 0], left[0]) - product(right[:, 1], left[1])
    imag_part = product(right[:, 0], left[1]) + product(right[:, 1], left[0])
    joined = jnp.stack([real_part, imag_part], axis=1).astype(BF16)
    groups = [list(range(c, 2 * chips, 2)) for c in range(2)]
    spread = lax.all_to_all(joined, "row", 0, 0, axis_index_groups=groups, tiled=True)
    t = spread.transpose(1, 2, 0, 3).reshape(2, spread.shape[2], -1)
    row_full = assemble(ring.gather(row_mats), owners)
    t = mix(t, row_full[0], True, False)
    t = mix(t, row_full[1], True, True)
    t = mix(t, row_full[2], True, False)
    back = t.reshape(2, t.shape[1], 2 * chips, -1).transpose(2, 0, 1, 3)
    back = lax.all_to_all(back, "row", 0, 0, tiled=True)
    t = back.transpose(1, 0, 2, 3).reshape(2, -1, back.shape[3])
    join_full = assemble(ring.gather(join_mats), owners)

    def apply(form, m, y):
        def p(a, b):
            return jnp.einsum(form, a, b, preferred_element_type=F32)

        return jnp.stack([p(m[0], y[0]) - p(m[1], y[1]), p(m[0], y[1]) + p(m[1], y[0])])

    t = apply("lj,ji->li", join_full[0], t).astype(BF16)
    out = apply("lj,ji->il", join_full[1], t)
    return out * (2.0 * cols) ** (-0.5)


def solution(mesh):
    in_specs = (
        P(None, ("cuts", "row"), None),
        P(None, ("cuts", "row"), None),
        P(None, None, None, "row", None),
        P("cuts"),
        P("cuts", None),
    )
    out_specs = P(None, ("cuts", "row"), None)
    body = functools.partial(shards, Ring(mesh))
    return jax.shard_map(body, mesh=mesh, in_specs=in_specs, out_specs=out_specs, check_vma=False)
```

```python
import functools

import jax
import jax.numpy as jnp
import numpy as np
from jax import lax
from jax.experimental import pallas as pl
from jax.experimental.pallas import tpu as pltpu
from jax.sharding import PartitionSpec as P


LEFT_SWEEPS = 3
RIGHT_SWEEPS = 2
F32 = jnp.float32
BF16 = jnp.bfloat16
NN = (((1,), (0,)), ((), ()))
NT = (((1,), (1,)), ((), ()))


def ring_order(mesh):
    devices = list(mesh.devices.reshape(-1, mesh.shape["row"])[0])
    chips = len(devices) // 2
    natural = list(range(chips))
    try:
        coords = [tuple(d.coords) for d in devices]
    except AttributeError:
        return natural
    spots = coords[::2]
    axes = [a for a in range(len(spots[0])) if len({s[a] for s in spots}) > 1]
    if len(axes) != 2:
        return natural
    short, long = sorted(axes, key=lambda a: len({s[a] for s in spots}))
    values = sorted({s[short] for s in spots})
    if len(values) != 2:
        return natural
    up = sorted((c for c in natural if spots[c][short] == values[0]), key=lambda c: spots[c][long])
    down = sorted((c for c in natural if spots[c][short] == values[1]), key=lambda c: -spots[c][long])
    return up + down


class Ring:
    def __init__(self, mesh):
        order = ring_order(mesh)
        self.chips = len(order)
        n = self.chips
        self.hop = [(2 * order[i], 2 * order[(i + 1) % n]) for i in range(n)]
        self.hop += [(2 * order[i] + 1, 2 * order[(i - 1) % n] + 1) for i in range(n)]
        self.swap = [(i, i ^ 1) for i in range(2 * n)]
        place = {chip: i for i, chip in enumerate(order)}
        table = np.zeros((2 * n, 2 * n), np.int32)
        for device in range(2 * n):
            chip, core = divmod(device, 2)
            for other in range(2):
                source = core ^ other
                sign = -1 if source == 0 else 1
                for step in range(n):
                    table[device, other * n + step] = 2 * order[(place[chip] + sign * step) % n] + source
        self.table = table

    def owners(self):
        return jnp.asarray(self.table)[lax.axis_index("row")]

    def same_core(self, shard):
        pieces = [shard]
        for _ in range(self.chips - 1):
            pieces.append(lax.ppermute(pieces[-1], "row", self.hop))
        return pieces

    def gather(self, shard):
        pieces = self.same_core(shard)
        return pieces + [lax.ppermute(p, "row", self.swap) for p in pieces]


def mix(x, matrix, transposed, strided):
    planes, rows, cols = x.shape
    width = matrix.shape[-1]
    groups = cols // width
    second = "dc" if transposed else "cd"
    if strided:
        view, form = x.reshape(planes, rows, width, groups), f"mcg,{second}->mdg"
    else:
        view, form = x.reshape(planes, rows, groups, width), f"mgc,{second}->mgd"

    def product(a, b):
        return jnp.einsum(form, a, b, preferred_element_type=F32)

    real_part = product(view[0], matrix[0]) - product(view[1], matrix[1])
    imag_part = product(view[0], matrix[1]) + product(view[1], matrix[0])
    return jnp.stack([real_part, imag_part]).reshape(x.shape).astype(BF16)


def permute(x, block_order):
    planes, rows, cols = x.shape
    blocks = block_order.shape[0]
    return jnp.take(x.reshape(planes, rows, blocks, cols // blocks), block_order, axis=2).reshape(x.shape)


def assemble(pieces, owners):
    order = jnp.zeros_like(owners).at[owners].set(jnp.arange(owners.shape[0], dtype=owners.dtype))
    stacked = jnp.take(jnp.stack(pieces), order, axis=0)
    count, matrices, planes, rows, width = stacked.shape
    return stacked.transpose(1, 2, 0, 3, 4).reshape(matrices, planes, count * rows, width)


def rows_of(plane, group, groups, rows):
    return (plane * groups + group) * rows


def lane_order(width, groups):
    source = lax.broadcasted_iota(jnp.int32, (width, width), 0)
    target = lax.broadcasted_iota(jnp.int32, (width, width), 1)
    sub = width // groups
    wanted = lax.rem(target, sub) * groups + lax.div(target, sub)
    return (source == wanted).astype(F32).astype(BF16)


def exchange_digits(src, dst, groups, rows, index=None):
    lane = lax.broadcasted_iota(jnp.int32, (rows, 128), 1)
    low = lane < 64

    def start(plane, group):
        if index is None:
            return rows_of(plane, group, groups, rows)
        return pl.multiple_of(plane * groups * rows + index(group) * rows, rows)

    for plane in range(2):
        for a in range(groups // 2):
            for b in range(groups // 2):
                even = src[pl.ds(start(plane, 2 * a), rows), b * 128 : (b + 1) * 128]
                odd = src[pl.ds(start(plane, 2 * a + 1), rows), b * 128 : (b + 1) * 128]
                lanes = slice(a * 128, (a + 1) * 128)
                first = rows_of(plane, 2 * b, groups, rows)
                dst[first : first + rows, lanes] = jnp.where(low, even, pltpu.roll(odd, 64, 1))
                second = rows_of(plane, 2 * b + 1, groups, rows)
                dst[second : second + rows, lanes] = jnp.where(low, pltpu.roll(even, 64, 1), odd)


def complex_mix(src, dst, mats, index, transposed):
    half = src.shape[0] // 2
    x = src[...].astype(BF16)
    turned = jnp.concatenate([-x[half:], x[:half]], axis=0)
    dims = NT if transposed else NN
    dst[...] = lax.dot_general(x, mats[index, 0], dims, preferred_element_type=F32) + lax.dot_general(
        turned, mats[index, 1], dims, preferred_element_type=F32
    )


def reorder(src, dst, order, transposed):
    dims = NT if transposed else NN
    dst[...] = lax.dot_general(src[...].astype(BF16), order[...], dims, preferred_element_type=F32)


def load_matrices(pieces, owners, chosen, mats, sems, rows):
    copies = []
    for at, piece in enumerate(pieces):
        where = pl.ds(pl.multiple_of(owners[at] * rows, rows), rows)
        source = piece.at[pl.ds(chosen, mats.shape[0])]
        copies.append(pltpu.make_async_copy(source, mats.at[:, :, where, :], sems.at[at]))
        copies[-1].start()
    return copies


def pick_kernel(orders, bits, branches, *refs):
    outs, sems = refs[:-1], refs[-1]
    copies = []
    for which, (order, out) in enumerate(zip(orders, outs)):
        for at, index in enumerate(order):
            source = branches.at[index, bits[index]]
            copies.append(pltpu.make_async_copy(source, out.at[at], sems.at[which, at]))
    for copy in copies:
        copy.start()
    for copy in copies:
        copy.wait()


def transpose(x):
    size = x.shape[1]
    across = lax.broadcasted_iota(jnp.int32, (size, size), 1)
    down = lax.broadcasted_iota(jnp.int32, (size, size), 0)
    same = (across == down).astype(F32).astype(BF16)
    return lax.dot_general(same, x.astype(BF16), NT, preferred_element_type=F32)


def turn_kernel(x, out, a, b, order):
    planes, rows, cols = x.shape
    width = order.shape[0]
    groups = cols // width
    order[...] = lane_order(width, groups)
    for plane in range(planes):
        for g in range(groups):
            at = rows_of(plane, g, groups, rows)
            a[at : at + rows, :] = x[plane, :, g * width : (g + 1) * width].astype(F32)
    reorder(a, b, order, False)
    exchange_digits(b, a, groups, rows)
    out[...] = a[...].astype(BF16)


def right_kernel(count, chosen, owners, perms, x, *refs):
    pieces = refs[:count]
    out_real, out_imag, mats, a, b, order, inverse, sems = refs[count:]
    planes = 2
    tall, width = x.shape
    rows, cols = out_real.shape
    groups = cols // width
    copies = load_matrices(pieces, owners, chosen, mats, sems, width // count)
    order[...] = lane_order(width, groups)
    for sweep in range(LEFT_SWEEPS):
        for g in range(groups):
            inverse[sweep, perms[sweep, g]] = g
    for copy in copies:
        copy.wait()
    complex_mix(x, b, mats, 0, False)
    exchange_digits(b, a, groups, rows)
    reorder(a, b, order, True)
    complex_mix(b, a, mats, 1, False)
    complex_mix(a, b, mats, 2, True)
    reorder(b, a, order, False)

    def block(group):
        return perms[LEFT_SWEEPS, perms[LEFT_SWEEPS + 1, inverse[2, inverse[1, group]]]]

    exchange_digits(a, b, groups, rows, block)
    complex_mix(b, a, mats, 3, True)
    exchange_digits(a, b, groups, rows)
    reorder(b, a, order, True)
    complex_mix(a, b, mats, 4, True)
    for plane, out in enumerate((out_real, out_imag)):
        for g in range(groups):
            at = pl.multiple_of(plane * groups * rows + inverse[0, g] * rows, rows)
            out[:, g * width : (g + 1) * width] = b[pl.ds(at, rows), :].astype(BF16)


def row_kernel(count, chosen, owners, x, *refs):
    pieces = refs[:count]
    out, mats, a, b, order, sems = refs[count:]
    groups, planes, rows, width = x.shape
    copies = load_matrices(pieces, owners, chosen, mats, sems, width // count)
    order[...] = lane_order(width, groups)
    for plane in range(planes):
        for g in range(groups):
            at = rows_of(plane, g, groups, rows)
            a[at : at + rows, :] = x[g, plane].astype(F32)
    for copy in copies:
        copy.wait()
    complex_mix(a, b, mats, 0, True)
    reorder(b, a, order, False)
    exchange_digits(a, b, groups, rows)
    complex_mix(b, a, mats, 1, True)
    exchange_digits(a, b, groups, rows)
    reorder(b, a, order, True)
    complex_mix(a, b, mats, 2, True)
    half = width // 2
    for plane in range(planes):
        for g in range(groups):
            at = rows_of(plane, g, groups, rows)
            for part in range(2):
                out[2 * g + part, plane] = b[at : at + rows, part * half : (part + 1) * half].astype(BF16)


def join_kernel(count, first, owners, own, other, *refs):
    pieces = refs[: 2 * count]
    out, stage, sems = refs[-3:]
    rows = pieces[0].shape[0]
    height, cols = own.shape[1:]
    tall = count * rows
    right = jnp.concatenate([piece[...] for piece in pieces], axis=0)
    sides = []
    for stem in (own, other):
        x = stem[...].reshape(2 * height, cols)
        product = lax.dot_general(right, x, NT, preferred_element_type=F32)
        real = product[:tall, :height] - product[tall:, height:]
        imag = product[tall:, :height] + product[:tall, height:]
        sides.append(jnp.concatenate([real, imag], axis=0).astype(BF16))
    core = lax.rem(owners[0], 2)
    low = jnp.where(core == 0, sides[0], sides[1])
    high = jnp.where(core == 0, sides[1], sides[0])
    copies = []
    for at in range(count):
        for plane in range(2):
            top = plane * tall + at * rows
            stage[at, plane, :, :height] = low[top : top + rows]
            stage[at, plane, :, height:] = high[top : top + rows]
        owner = lax.div(owners[first + at], 2)
        copies.append(pltpu.make_async_copy(stage.at[at], out.at[owner], sems.at[at]))
        copies[-1].start()
    for copy in copies:
        copy.wait()


def last_kernel(count, chosen, scale, owners, x, *refs):
    pieces = refs[:count]
    out, mats, a, b, sems = refs[count:]
    _, planes, rows, width = x.shape
    copies = load_matrices(pieces, owners, chosen, mats, sems, mats.shape[2] // count)
    for plane in range(planes):
        for at in range(count):
            b[at * rows : (at + 1) * rows, plane * width : (plane + 1) * width] = x[at, plane].astype(F32)
    a[...] = transpose(b[...])
    for copy in copies:
        copy.wait()
    complex_mix(a, b, mats, 0, True)
    complex_mix(b, a, mats, 1, True)
    for plane in range(planes):
        out[plane] = a[plane * width : (plane + 1) * width, :] * scale


SMEM = pl.BlockSpec(memory_space=pltpu.SMEM)
VMEM = pl.BlockSpec(memory_space=pltpu.VMEM)
ANY = pl.BlockSpec(memory_space=pltpu.HBM)


def kernel_params(limit=54 * 1024 * 1024):
    return pltpu.CompilerParams(vmem_limit_bytes=limit)


def estimate(flops, nbytes):
    return pl.CostEstimate(flops=int(flops), bytes_accessed=int(nbytes), transcendentals=0)


def pick(orders, bits, branches):
    planes, rows, width = branches.shape[2:]
    return pl.pallas_call(
        functools.partial(pick_kernel, orders),
        out_shape=[jax.ShapeDtypeStruct((len(order), planes, rows, width), BF16) for order in orders],
        in_specs=[SMEM, ANY],
        out_specs=[VMEM] * len(orders),
        scratch_shapes=[pltpu.SemaphoreType.DMA((len(orders), max(map(len, orders))))],
        compiler_params=kernel_params(),
        name="pick",
    )(bits, branches)


def turn(x, width):
    planes, height, cols = x.shape
    tall = planes * height * cols // width
    return pl.pallas_call(
        turn_kernel,
        out_shape=jax.ShapeDtypeStruct((tall, width), BF16),
        in_specs=[VMEM],
        out_specs=VMEM,
        scratch_shapes=[
            pltpu.VMEM((tall, width), F32),
            pltpu.VMEM((tall, width), F32),
            pltpu.VMEM((width, width), BF16),
        ],
        cost_estimate=estimate(2 * tall * width * width, 4 * tall * width),
        compiler_params=kernel_params(),
        name="turn",
    )(x)


def mix_right(owners, perms, x, cols, chosen, matrices, pieces):
    count = len(pieces)
    tall, width = x.shape
    height = tall * width // (2 * cols)
    return pl.pallas_call(
        functools.partial(right_kernel, count, chosen),
        out_shape=[jax.ShapeDtypeStruct((height, cols), BF16)] * 2,
        in_specs=[SMEM, SMEM, VMEM] + [ANY] * count,
        out_specs=[VMEM, VMEM],
        scratch_shapes=[
            pltpu.VMEM((matrices, 2, width, width), BF16),
            pltpu.VMEM((tall, width), F32),
            pltpu.VMEM((tall, width), F32),
            pltpu.VMEM((width, width), BF16),
            pltpu.SMEM((LEFT_SWEEPS, cols // width), jnp.int32),
            pltpu.SemaphoreType.DMA((count,)),
        ],
        cost_estimate=estimate(4 * tall * width * width * matrices * 2, 2 * matrices * 2 * width * width),
        compiler_params=kernel_params(),
        name="mix_right",
    )(owners, perms, x, *pieces)


def mix_rows(owners, x, chosen, matrices, pieces):
    count = len(pieces)
    width = pieces[0].shape[3]
    groups, planes, height, _ = x.shape
    tall = planes * height * groups
    return pl.pallas_call(
        functools.partial(row_kernel, count, chosen),
        out_shape=jax.ShapeDtypeStruct((2 * groups, planes, height, width // 2), BF16),
        in_specs=[SMEM, VMEM] + [ANY] * count,
        out_specs=VMEM,
        scratch_shapes=[
            pltpu.VMEM((matrices, 2, width, width), BF16),
            pltpu.VMEM((tall, width), F32),
            pltpu.VMEM((tall, width), F32),
            pltpu.VMEM((width, width), BF16),
            pltpu.SemaphoreType.DMA((count,)),
        ],
        cost_estimate=estimate(4 * tall * width * width * matrices * 2, 2 * matrices * 2 * width * width),
        compiler_params=kernel_params(),
        name="mix_rows",
    )(owners, x, *pieces)


def join(owners, first, chips, own, other, real, imag, before=()):
    count = len(real)
    rows, cols = real[0].shape
    height = own.shape[1]
    return pl.pallas_call(
        functools.partial(join_kernel, count, first),
        out_shape=jax.ShapeDtypeStruct((chips, 2, rows, 2 * height), BF16),
        in_specs=[SMEM, VMEM, VMEM] + [VMEM] * (2 * count) + [ANY] * len(before),
        out_specs=ANY,
        scratch_shapes=[
            pltpu.VMEM((count, 2, rows, 2 * height), BF16),
            pltpu.SemaphoreType.DMA((count,)),
        ],
        input_output_aliases={3 + 2 * count: 0} if before else {},
        cost_estimate=estimate(16 * count * rows * cols * height, 2 * 2 * cols * (2 * height + count * rows)),
        compiler_params=kernel_params(24 * 1024 * 1024),
        name="join",
    )(owners, own, other, *real, *imag, *before)


def mix_last(owners, scale, x, chosen, matrices, pieces):
    count = len(pieces)
    full = pieces[0].shape[3]
    _, planes, _, width = x.shape
    return pl.pallas_call(
        functools.partial(last_kernel, count, chosen, scale),
        out_shape=jax.ShapeDtypeStruct((planes, width, full), F32),
        in_specs=[SMEM, VMEM] + [ANY] * count,
        out_specs=VMEM,
        scratch_shapes=[
            pltpu.VMEM((matrices, 2, full, full), BF16),
            pltpu.VMEM((planes * width, full), F32),
            pltpu.VMEM((full, planes * width), F32),
            pltpu.SemaphoreType.DMA((count,)),
        ],
        cost_estimate=estimate(4 * planes * width * full * full * matrices, 2 * matrices * 2 * full * full),
        compiler_params=kernel_params(),
        name="mix_last",
    )(owners, x, *pieces)


def fits_kernels(ring, left_stem, right_stem, branches):
    rows, width = branches.shape[3:]
    groups = left_stem.shape[2] // width
    return (
        rows % 16 == 0
        and right_stem.shape[1] % 16 == 0
        and 2 * left_stem.shape[1] == width
        and ring.chips == groups
        and width // groups == 64
        and groups % 2 == 0
        and 2 * ring.chips * right_stem.shape[1] == width
    )


def shards(ring, left_stem, right_stem, branches, slice_bits, perms):
    if fits_kernels(ring, left_stem, right_stem, branches):
        return shards_kernels(ring, left_stem, right_stem, branches, slice_bits, perms)
    return shards_xla(ring, left_stem, right_stem, branches, slice_bits, perms)


def tie(*values):
    return lax.optimization_barrier(values)


def shards_kernels(ring, left_stem, right_stem, branches, slice_bits, perms):
    cols = left_stem.shape[2]
    width = branches.shape[4]
    chips = ring.chips
    owners = ring.owners()

    streams = pick(((6, 8, 4, 2, 0), (1, 3, 5, 7, 9)), slice_bits, branches)
    left_other = lax.ppermute(left_stem, "row", ring.swap)
    turned = turn(right_stem, width)
    same = [[s] for s in streams]
    swapped = [[], []]
    for step in range(chips - 1):
        for which in range(2):
            arrived = lax.ppermute(same[which][-1], "row", ring.hop)
            crossed = lax.ppermute(same[which][-1], "row", ring.swap)
            arrived, crossed = tie(arrived, crossed)
            if which == 0 and step > 0:
                arrived, _ = tie(arrived, same[1][-1])
            if which == 0 and step == 1:
                arrived, owners = tie(arrived, owners)
            if which == 0 and step == 2:
                arrived, turned = tie(arrived, turned)
            if which == 0 and step == 3:
                arrived, left_other = tie(arrived, left_other)
            same[which].append(arrived)
            swapped[which].append(crossed)
    for which in range(2):
        swapped[which].append(lax.ppermute(same[which][-1], "row", ring.swap))
    col_pieces, row_pieces = [a + b for a, b in zip(same, swapped)]

    shard = mix_right(owners, perms, turned, cols, 0, 5, col_pieces)
    right = [[plane] for plane in shard]
    ahead = swapped[1][-1]
    half = chips // 2
    for step in range(chips - 1):
        if step == 2:
            right[0][-1], _ = tie(right[0][-1], ahead)
        for plane in right:
            plane.append(lax.ppermute(plane[-1], "row", ring.hop))
    held = [plane[:half] for plane in right]
    held[0][0], *_ = tie(held[0][0], right[0][-2], right[1][-2])
    joined = join(owners, 0, chips, left_stem, left_other, *held)
    joined = join(owners, half, chips, left_stem, left_other, *[p[half:] for p in right], (joined,))

    groups = [list(range(c, 2 * chips, 2)) for c in range(2)]
    spread = lax.all_to_all(joined, "row", 0, 0, axis_index_groups=groups, tiled=True)
    mixed = mix_rows(owners, spread, 0, 3, row_pieces)
    back = lax.all_to_all(mixed, "row", 0, 0, tiled=True)
    return mix_last(owners, (2.0 * cols) ** (-0.5), back, 3, 2, row_pieces)


def shards_xla(ring, left_stem, right_stem, branches, slice_bits, perms):
    cols = left_stem.shape[2]
    chips = ring.chips
    owners = ring.owners()
    pick = (slice_bits == 0)[:, None, None, None]
    chosen = jnp.where(pick, branches[:, 0], branches[:, 1])

    col_mats = jnp.stack([chosen[i] for i in (6, 8, 4, 2, 0)])
    row_mats = jnp.stack([chosen[i] for i in (1, 3, 5)])
    join_mats = jnp.stack([chosen[i] for i in (7, 9)])

    left_other = lax.ppermute(left_stem, "row", ring.swap)
    mats = assemble(ring.gather(col_mats), owners)
    inverse = jnp.argsort(perms, axis=1)
    v = mix(right_stem, mats[0], False, True)
    v = permute(v, perms[3])
    v = mix(v, mats[1], False, False)
    v = permute(v, perms[4])
    v = permute(v, inverse[2])
    v = mix(v, mats[2], True, False)
    v = permute(v, inverse[1])
    v = mix(v, mats[3], True, True)
    v = permute(v, inverse[0])
    v = mix(v, mats[4], True, False)

    pieces = ring.same_core(v)
    core = lax.axis_index("row") % 2
    first = jnp.where(core == 0, left_stem, left_other)
    second = jnp.where(core == 0, left_other, left_stem)
    left = jnp.concatenate([first, second], axis=1)
    order = jnp.zeros((chips,), jnp.int32).at[owners[:chips] // 2].set(jnp.arange(chips, dtype=jnp.int32))
    right = jnp.take(jnp.stack(pieces), order, axis=0)

    def product(a, b):
        return jnp.einsum("qjk,ik->qji", a, b, preferred_element_type=F32)

    real_part = product(right[:, 0], left[0]) - product(right[:, 1], left[1])
    imag_part = product(right[:, 0], left[1]) + product(right[:, 1], left[0])
    joined = jnp.stack([real_part, imag_part], axis=1).astype(BF16)
    groups = [list(range(c, 2 * chips, 2)) for c in range(2)]
    spread = lax.all_to_all(joined, "row", 0, 0, axis_index_groups=groups, tiled=True)
    t = spread.transpose(1, 2, 0, 3).reshape(2, spread.shape[2], -1)
    row_full = assemble(ring.gather(row_mats), owners)
    t = mix(t, row_full[0], True, False)
    t = mix(t, row_full[1], True, True)
    t = mix(t, row_full[2], True, False)
    back = t.reshape(2, t.shape[1], 2 * chips, -1).transpose(2, 0, 1, 3)
    back = lax.all_to_all(back, "row", 0, 0, tiled=True)
    t = back.transpose(1, 0, 2, 3).reshape(2, -1, back.shape[3])
    join_full = assemble(ring.gather(join_mats), owners)

    def apply(form, m, y):
        def p(a, b):
            return jnp.einsum(form, a, b, preferred_element_type=F32)

        return jnp.stack([p(m[0], y[0]) - p(m[1], y[1]), p(m[0], y[1]) + p(m[1], y[0])])

    t = apply("lj,ji->li", join_full[0], t).astype(BF16)
    out = apply("lj,ji->il", join_full[1], t)
    return out * (2.0 * cols) ** (-0.5)


def solution(mesh):
    in_specs = (
        P(None, ("cuts", "row"), None),
        P(None, ("cuts", "row"), None),
        P(None, None, None, "row", None),
        P("cuts"),
        P("cuts", None),
    )
    out_specs = P(None, ("cuts", "row"), None)
    body = functools.partial(shards, Ring(mesh))
    return jax.shard_map(body, mesh=mesh, in_specs=in_specs, out_specs=out_specs, check_vma=False)
```
